256 devices in a mesh: section: 8 (over z), rep: 32 (over y, x, core).
Axes of the slice: x: 4, y: 4, z: 8, core: 2. Of those that a mesh axis runs over, the one named last changes fastest.
Arguments:
- features: bfloat16 [49152, 512], P('rep'), may hold values from -6 to 6
- stale_states: bfloat16 [16, 16384, 512], P('section', 'rep'), may hold values from -6 to 6
- tile_values: bfloat16 [96, 2, 4, 2, 128, 128], P('rep'), may hold values from -0.25 to 0.25
- tile_index: int32 [96, 2, 4, 2], P('rep'), may hold values from 0 to 3
- tile_count: int32 [96, 2, 4], P('rep'), may hold values from 1 to 2
- weights: bfloat16 [16, 512, 512], P('section'), may hold values from -0.25 to 0.25
- cotangent: bfloat16 [49152, 512], P('rep'), may hold values from -6 to 6
Outputs:
- section_states: bfloat16 [8, 49152, 512], P('section', 'rep')
- section_grads: bfloat16 [8, 49152, 512], P('section', 'rep')
- weight_grads: float32 [16, 512, 512], P('section', 'rep')
The draws below stay inside these ranges and needn't reach their ends.
Inputs may be any that keep to these rules, and one draw needn't show every extreme that they name: `tile_index`: tile slots name tiles of their own partition's stale nodes. `tile_count`: slots at or beyond the count are ignored.
All inputs are finite; a program needn't handle non-finite values.
Results may differ from the reference program's by a relative error of at most 0.02.
Values may be sent and summed in bfloat16 or wider, within the bound.
No kernel may reach another device: no remote copies, remote signals or barrier semaphores. Data moves between devices by JAX's collectives and lax.ppermute only.
A program may use at most 64 MiB of HBM per device.

```python
import math
import jax
import jax.numpy as jnp
from jax import lax

WIDTH = 512
SECTION_LAYERS = 2
GROUP = 512
TILE = 128
RELATIONS = 2
TILES_ROW = 2
GROUPS = 3
STALE_GROUPS = 1
TILE_ROWS = 4
LAYERS = 16
NODES = 49152
STALE_NODES = 16384
ITEMS = 96
N_SECTION = 8
N_REP = 32


def plant(array, stream_key, smallest, high):
    longest = array.shape.index(max(array.shape))
    spots = []
    for shift in (0, 1):
        where = [jax.random.randint(jax.random.fold_in(stream_key, axis), (), 0, length) for axis, length in enumerate(array.shape)]
        where[longest] = (where[longest] + shift) % array.shape[longest]
        spots.append(tuple(where))
    return array.at[spots[0]].set(smallest).at[spots[1]].set(high)


def shard_levels(own_key, shape, shards, smallest, top_value):
    gain = 1.0
    for dim, parts in shards:
        draws = jax.random.uniform(jax.random.fold_in(jax.random.fold_in(own_key, 6), dim), (parts,), jnp.float32, smallest / len(shards), top_value / len(shards))
        gain = gain * jnp.repeat(jnp.exp(draws), shape[dim] // parts).reshape((-1,) + (1,) * (len(shape) - 1 - dim))
    return gain


def normal_values(rng, extent, deviation, most, shards=(), held_as=jnp.bfloat16):
    level = shard_levels(rng, extent, shards, -0.22, 0.18) if shards else 1.0
    array = jax.random.normal(rng, extent, jnp.float32) * deviation * level
    return jnp.minimum(jnp.maximum(array, -most), most).astype(held_as)


def setup_inputs(seed: int = 0) -> dict:
    splits = jax.random.split(jax.random.key(seed), 8)
    features = normal_values(splits[0], (NODES, WIDTH), 1.0, 6.0, ((0, 32),))
    stale_states = normal_values(splits[1], (LAYERS, STALE_NODES, WIDTH), 1.0, 6.0, ((0, 8), (1, 32)))
    tile_values = normal_values(splits[2], (ITEMS, RELATIONS, TILE_ROWS, TILES_ROW, TILE, TILE), (RELATIONS * TILES_ROW * TILE) ** -0.5, 0.25, ((0, 32),))
    tile_index = plant(jax.random.randint(splits[3], (ITEMS, RELATIONS, TILE_ROWS, TILES_ROW), 0, STALE_GROUPS * TILE_ROWS), jax.random.fold_in(splits[3], 1), 0, (STALE_GROUPS * TILE_ROWS) - 1).astype(jnp.int32)
    tile_count = plant(jax.random.randint(splits[4], (ITEMS, RELATIONS, TILE_ROWS), 1, TILES_ROW + 1), jax.random.fold_in(splits[4], 1), 1, TILES_ROW).astype(jnp.int32)
    weights = normal_values(splits[5], (LAYERS, WIDTH, WIDTH), WIDTH ** -0.5, 0.25, ((0, 8),))
    cotangent = normal_values(splits[6], (NODES, WIDTH), 1.0, 6.0, ((0, 32),))
    return dict(features=features, stale_states=stale_states, tile_values=tile_values, tile_index=tile_index, tile_count=tile_count, weights=weights, cotangent=cotangent)


mix_alpha = 0.1
theta_scale = 0.5
residual_scale = 0.5 ** 0.5


def aggregate(layer_stale, tile_values, tile_index, tile_count):
    gathered = layer_stale.reshape(-1, TILE, layer_stale.shape[-1])[tile_index]
    slot_ids = lax.broadcasted_iota(jnp.int32, tile_index.shape, 2)
    live = (slot_ids < tile_count[..., None]).astype(jnp.float32)
    masked = tile_values.astype(jnp.float32) * live[..., None, None]
    summed = jnp.einsum("rtkab,rtkbf->taf", masked, gathered.astype(jnp.float32), precision=lax.Precision.HIGHEST)
    return summed.reshape(-1, layer_stale.shape[-1])


def layer_forward(states_in, anchor, layer_stale, tile_values, tile_index, tile_count, weight, beta):
    summed = aggregate(layer_stale, tile_values, tile_index, tile_count)
    mixed = (1.0 - mix_alpha) * (states_in.astype(jnp.float32) + summed) + mix_alpha * anchor.astype(jnp.float32)
    rounded = mixed.astype(jnp.bfloat16)
    before = (1.0 - beta) * mixed + beta * jnp.dot(rounded, weight, preferred_element_type=jnp.float32)
    result = ((states_in.astype(jnp.float32) + jax.nn.silu(before)) * residual_scale).astype(jnp.bfloat16)
    return result, rounded, before


def layer_backward(upstream, rounded, before, weight, beta):
    sigma_v = jax.nn.sigmoid(before)
    d_before = residual_scale * upstream * sigma_v * (1.0 + before * (1.0 - sigma_v))
    d_scaled = (beta * d_before).astype(jnp.bfloat16)
    weight_term = jnp.dot(rounded.T, d_scaled, preferred_element_type=jnp.float32)
    d_mixed = (1.0 - beta) * d_before + jnp.dot(d_scaled, weight.T, preferred_element_type=jnp.float32)
    return residual_scale * upstream + (1.0 - mix_alpha) * d_mixed, weight_term


def reference(features, stale_states, tile_values, tile_index, tile_count, weights, cotangent):
    item_total = N_REP * GROUPS
    betas = [math.log(theta_scale / (depth + 1) + 1.0) for depth in range(LAYERS)]

    def one_item(total_grad, item):
        replica = item // GROUPS
        start = (item * GROUP).astype(jnp.int32)
        anchor = lax.dynamic_slice_in_dim(features, start, GROUP, 0)
        item_stale = lax.dynamic_slice_in_dim(stale_states, (replica * STALE_GROUPS * GROUP).astype(jnp.int32), STALE_GROUPS * GROUP, 1)
        item_values = lax.dynamic_index_in_dim(tile_values, item, 0, keepdims=False)
        item_index = lax.dynamic_index_in_dim(tile_index, item, 0, keepdims=False)
        item_count = lax.dynamic_index_in_dim(tile_count, item, 0, keepdims=False)
        states_in = anchor
        saved = []
        section_out = []
        for depth in range(LAYERS):
            states_in, rounded, before = layer_forward(states_in, anchor, item_stale[depth], item_values, item_index, item_count, weights[depth], betas[depth])
            saved.append((rounded, before))
            if (depth + 1) % SECTION_LAYERS == 0:
                section_out.append(states_in)
        upstream = lax.dynamic_slice_in_dim(cotangent, start, GROUP, 0).astype(jnp.float32)
        grads = [None] * LAYERS
        section_grad = [None] * N_SECTION
        for depth in reversed(range(LAYERS)):
            upstream, weight_term = layer_backward(upstream, saved[depth][0], saved[depth][1], weights[depth], betas[depth])
            grads[depth] = weight_term
            if depth % SECTION_LAYERS == 0:
                rounded_grad = lax.optimization_barrier(upstream.astype(jnp.bfloat16))
                section_grad[depth // SECTION_LAYERS] = rounded_grad
                upstream = rounded_grad.astype(jnp.float32)
        return total_grad + jnp.stack(grads), (jnp.stack(section_out), jnp.stack(section_grad))

    total_grad, (state_stack, grad_stack) = lax.scan(one_item, jnp.zeros((LAYERS, WIDTH, WIDTH), jnp.float32), jnp.arange(item_total, dtype=jnp.int32))
    section_states = jnp.transpose(state_stack, (1, 0, 2, 3)).reshape(N_SECTION, item_total * GROUP, WIDTH)
    section_grads = jnp.transpose(grad_stack, (1, 0, 2, 3)).reshape(N_SECTION, item_total * GROUP, WIDTH)
    return section_states, section_grads, total_grad / N_REP
```

```python
import functools
import math

import jax
import jax.numpy as jnp
from jax import lax
from jax.experimental import pallas as pl
from jax.experimental.pallas import tpu as pltpu
from jax.sharding import PartitionSpec as P

TILE = 128
STREAMS = 3
GRANT = 8 << 20

mix_alpha = 0.1
theta_scale = 0.5
residual_scale = 0.5**0.5


def dot_f32(a, b):
    return jnp.dot(a, b, preferred_element_type=jnp.float32)


def dot_t(a, b):
    return lax.dot_general(a, b, (((0,), (0,)), ((), ())), preferred_element_type=jnp.float32)


class Plan:
    def __init__(self, tick, stream, sections, steps):
        last_forward = sections - 1 + 2 * (steps - 1)
        first_backward = sections
        self.tick = tick
        self.stream = stream
        self.sections = sections
        self.steps = steps
        self.forward = tick <= last_forward
        self.backward = tick >= first_backward
        self.first_mix = tick == 0
        ahead = tick // 2 + 1
        self.next_mix = ahead if ahead < steps else None
        behind = (tick - 2 * sections) // 2
        self.weight = behind if (stream == STREAMS - 1 and 0 <= behind < steps - 1) else None
        reads, writes = set(), set()
        if self.first_mix or self.next_mix is not None:
            reads |= {"index", "count", "features", "stale", "tiles"}
            writes |= {"mix"}
        if self.forward:
            reads |= {"features", "weights", "mix"}
            writes |= {"slope", "rounded", "states"}
        if self.backward:
            reads |= {"cotangent", "weights_t", "slope"}
            writes |= {"scaled", "grads"}
        if self.weight is not None:
            reads |= {"rounded", "scaled"}
            writes |= {"total"}
        self.flush = self.weight == 0
        if self.flush:
            reads |= {"states"}
            writes |= {"states_out"}
        self.reads, self.writes = reads, writes


def compute_mix(ref, chunk, per_group):
    index, count = ref["index"], ref["count"]
    item, row = divmod(chunk, per_group)
    _, relations, rows_of, slots, _, _ = ref["tiles"].shape
    values, picks = [], []
    for r in range(relations):
        for k in range(slots):
            live = k < count[(item * relations + r) * rows_of + row]
            tile = ref["tiles"][item, r, row, k]
            values.append(jnp.where(live, tile, jnp.zeros_like(tile)))
            start = index[((item * relations + r) * rows_of + row) * slots + k] * TILE
            picks.append(pl.multiple_of(start, TILE))
    values = jnp.concatenate(values, axis=1)
    rows = slice(chunk * TILE, (chunk + 1) * TILE)
    anchor = mix_alpha * ref["features"][rows, :].astype(jnp.float32)
    for depth in range(ref["stale"].shape[0]):
        gathered = jnp.concatenate([ref["stale"][depth, pl.ds(s, TILE), :] for s in picks], axis=0)
        ref["mix"][depth, rows, :] = (1.0 - mix_alpha) * dot_f32(values, gathered) + anchor


def forward_chunk(ref, rows, section, beta, recv, send):
    anchor = ref["features"][rows, :]
    current = jnp.where(section == 0, anchor, recv[...])
    depths = ref["weights"].shape[0]
    for depth in range(depths):
        hidden = current.astype(jnp.float32)
        mixed = (1.0 - mix_alpha) * hidden + ref["mix"][depth, rows, :]
        rounded = mixed.astype(jnp.bfloat16)
        ref["rounded"][depth, rows, :] = rounded
        before = (1.0 - beta[depth]) * mixed + beta[depth] * dot_f32(rounded, ref["weights"][depth])
        sigma = 0.5 * jnp.tanh(0.5 * before) + 0.5
        silu = before * sigma
        current = ((hidden + silu) * residual_scale).astype(jnp.bfloat16)
        slope = residual_scale * (sigma + silu * (1.0 - sigma))
        ref["slope"][depth, rows, :] = slope.astype(jnp.bfloat16)
    ref["states"][rows, :] = current
    send[...] = current


def backward_chunk(ref, rows, section, sections, beta, recv, send):
    last = ref["cotangent"][rows, :]
    upstream = jnp.where(section == sections - 1, last, recv[...]).astype(jnp.float32)
    depths = ref["weights_t"].shape[0]
    for depth in reversed(range(depths)):
        d_before = upstream * ref["slope"][depth, rows, :].astype(jnp.float32)
        d_scaled = (beta[depth] * d_before).astype(jnp.bfloat16)
        ref["scaled"][depth, rows, :] = d_scaled
        d_mixed = (1.0 - beta[depth]) * d_before + dot_f32(d_scaled, ref["weights_t"][depth])
        upstream = residual_scale * upstream + (1.0 - mix_alpha) * d_mixed
    grad = upstream.astype(jnp.bfloat16)
    ref["grads"][rows, :] = grad
    send[...] = grad


def betas_of(section, sections, depths):
    beta = []
    for depth in range(depths):
        value = jnp.float32(math.log(theta_scale / (depth + 1) + 1.0))
        for s in range(1, sections):
            layer = s * depths + depth
            value = jnp.where(
                section == s, jnp.float32(math.log(theta_scale / (layer + 1) + 1.0)), value
            )
        beta.append(value)
    return beta


def tick_kernel(plan, depths, per_group, names_in, names_out, *refs):
    recv = refs[0]
    ref = dict(zip(names_in, refs[1 : 1 + len(names_in)]))
    outs = refs[1 + len(names_in) :]
    send = outs[0]
    ref.update(zip(names_out, outs[1 : 1 + len(names_out)]))
    section = lax.axis_index("section")
    beta = betas_of(section, plan.sections, depths)
    tick, stream = plan.tick, plan.stream
    own = lax.rem(section + tick, 2) == 0

    if plan.first_mix:
        compute_mix(ref, stream, per_group)
    if plan.next_mix is not None:

        @pl.when(jnp.logical_not(own))
        def _():
            compute_mix(ref, plan.next_mix * STREAMS + stream, per_group)

    def rows_of(step):
        return pl.ds(pl.multiple_of((step * STREAMS + stream) * TILE, TILE), TILE)

    if plan.forward:
        twice = tick - section

        @pl.when(own & (twice >= 0) & (twice < 2 * plan.steps))
        def _():
            forward_chunk(ref, rows_of(lax.div(twice, 2)), section, beta, recv, send)

    if plan.backward:
        twice_back = tick - (2 * plan.sections - 1) + section

        @pl.when(jnp.logical_not(own) & (twice_back >= 0) & (twice_back < 2 * plan.steps))
        def _():
            backward_chunk(
                ref, rows_of(lax.div(twice_back, 2)), section, plan.sections, beta, recv, send
            )

    if plan.weight is not None:
        size = STREAMS * TILE
        rows = slice(plan.weight * size, (plan.weight + 1) * size)

        @pl.when(own)
        def _():
            if plan.flush:
                copy = pltpu.make_async_copy(ref["states"], ref["states_out"], outs[-1])
                copy.start()
            for depth in range(ref["total"].shape[0]):
                term = dot_t(ref["rounded"][depth, rows, :], ref["scaled"][depth, rows, :])
                if plan.weight == 0:
                    ref["total"][depth] = term
                else:
                    ref["total"][depth] += term
            if plan.flush:
                copy.wait()


def finish_kernel(rows, reps, rounded, scaled, total, grads, out, grads_out, sem):
    copy = pltpu.make_async_copy(grads, grads_out, sem)
    copy.start()
    depths, width, _ = total.shape
    share = width // reps
    for depth in range(depths):
        term = dot_t(rounded[depth, rows, :], scaled[depth, rows, :])
        full = (total[depth] + term).astype(jnp.bfloat16)
        for r in range(reps):
            start = (r * depths + depth) * share
            out[start : start + share, :] = full[r * share : (r + 1) * share, :]
    copy.wait()


def transpose_kernel(w, out):
    for depth in range(w.shape[0]):
        out[depth] = w[depth].T


vmem = functools.partial(pl.BlockSpec, memory_space=pltpu.VMEM)


def spec_of(name):
    spaces = {"index": pltpu.SMEM, "count": pltpu.SMEM, "states_out": pl.ANY}
    return pl.BlockSpec(memory_space=spaces.get(name, pltpu.VMEM))


def body(features, stale_states, tile_values, tile_index, tile_count, weights, cotangent):
    sections = lax.axis_size("section")
    reps = lax.axis_size("rep")
    depths = weights.shape[0]
    nodes, width = features.shape
    per_group = tile_values.shape[2]
    steps = nodes // (STREAMS * TILE)
    ticks = 2 * sections - 2 + 2 * steps

    buffers = {
        "features": features,
        "stale": stale_states,
        "tiles": tile_values,
        "weights": weights,
        "index": tile_index.reshape(-1),
        "count": tile_count.reshape(-1),
        "cotangent": cotangent,
    }
    buffers["weights_t"] = pl.pallas_call(
        transpose_kernel,
        out_shape=jax.ShapeDtypeStruct(weights.shape, weights.dtype),
        in_specs=[vmem()],
        out_specs=vmem(),
        compiler_params=pltpu.CompilerParams(vmem_limit_bytes=GRANT),
        name="transpose",
    )(weights)
    low, wide = jnp.bfloat16, jnp.float32
    shapes = {
        "mix": jax.ShapeDtypeStruct((depths, nodes, width), wide),
        "slope": jax.ShapeDtypeStruct((depths, nodes, width), low),
        "rounded": jax.ShapeDtypeStruct((depths, nodes, width), low),
        "scaled": jax.ShapeDtypeStruct((depths, nodes, width), low),
        "states": jax.ShapeDtypeStruct((nodes, width), low),
        "states_out": jax.ShapeDtypeStruct((nodes, width), low),
        "grads": jax.ShapeDtypeStruct((nodes, width), low),
        "total": jax.ShapeDtypeStruct((depths, width, width), wide),
    }
    parcel = jax.ShapeDtypeStruct((TILE, width), low)
    exchange = [
        [(i, i ^ 1) for i in range(sections)],
        [((i + 1) % sections, ((i ^ 1) + 1) % sections) for i in range(sections)],
    ]
    received = [features[:TILE]] * STREAMS
    for tick in range(ticks):
        for stream in range(STREAMS):
            plan = Plan(tick, stream, sections, steps)
            names_out = sorted(plan.writes)
            names_in = sorted((plan.reads | plan.writes) & set(buffers))
            aliases = {1 + names_in.index(n): 1 + names_out.index(n) for n in names_out if n in buffers}
            results = pl.pallas_call(
                functools.partial(tick_kernel, plan, depths, per_group, names_in, names_out),
                out_shape=[parcel] + [shapes[n] for n in names_out],
                in_specs=[vmem()] + [spec_of(n) for n in names_in],
                out_specs=[vmem()] + [spec_of(n) for n in names_out],
                scratch_shapes=[pltpu.SemaphoreType.DMA] if plan.flush else [],
                input_output_aliases=aliases,
                compiler_params=pltpu.CompilerParams(vmem_limit_bytes=GRANT),
                cost_estimate=pl.CostEstimate(
                    flops=4 * TILE * width * width, bytes_accessed=1 << 20, transcendentals=0
                ),
                name=f"tick{tick}_{stream}",
            )(received[stream], *[buffers[n] for n in names_in])
            buffers.update(zip(names_out, results[1:]))
            if tick + 1 < ticks:
                received[stream] = lax.ppermute(results[0], "section", exchange[tick % 2])

    size = STREAMS * TILE
    terms, grads_out = pl.pallas_call(
        functools.partial(finish_kernel, slice((steps - 1) * size, steps * size), reps),
        out_shape=[jax.ShapeDtypeStruct((depths * width, width), low), shapes["grads"]],
        in_specs=[vmem()] * 4,
        out_specs=[vmem(), pl.BlockSpec(memory_space=pl.ANY)],
        scratch_shapes=[pltpu.SemaphoreType.DMA],
        compiler_params=pltpu.CompilerParams(vmem_limit_bytes=GRANT),
        name="finish",
    )(buffers["rounded"], buffers["scaled"], buffers["total"], buffers["grads"])
    parts = lax.all_to_all(
        terms.reshape(reps, -1, width), "rep", split_axis=0, concat_axis=0, tiled=True
    )
    weight_grads = parts.astype(jnp.float32).sum(0) * (1.0 / reps)
    return (
        buffers["states_out"][None],
        grads_out[None],
        weight_grads.reshape(depths, width // reps, width),
    )


def solution(mesh):
    return jax.shard_map(
        body,
        mesh=mesh,
        in_specs=(
            P("rep", None),
            P("section", "rep", None),
            P("rep", None, None, None, None, None),
            P("rep", None, None, None),
            P("rep", None, None),
            P("section", None, None),
            P("rep", None),
        ),
        out_specs=(P("section", "rep", None), P("section", "rep", None), P("section", "rep", None)),
        check_vma=False,
    )
```

```python
import functools
import math

import jax
import jax.numpy as jnp
from jax import lax
from jax.experimental import pallas as pl
from jax.experimental.pallas import tpu as pltpu
from jax.sharding import PartitionSpec as P

TILE = 128
PHASES = (0, 1, 0)
STREAMS = len(PHASES)
GRANT = 8 << 20

mix_alpha = 0.1
theta_scale = 0.5
residual_scale = 0.5**0.5


(
    FEATURES_HBM,
    STALE_HBM,
    TILES_HBM,
    WEIGHTS_HBM,
    COTANGENT_HBM,
    INDEX_HBM,
    COUNT_HBM,
    FEATURES,
    STALE,
    TILES,
    WEIGHTS,
    WEIGHTS_T,
    COTANGENT,
    MIX,
    SLOPE,
    ROUNDED,
    SCALED,
    STATES,
    STATES_OUT,
    GRADS,
    TOTAL,
    INDEX_SMEM,
    COUNT_SMEM,
    PLACED,
) = range(24)

ARGS_HBM = {
    FEATURES_HBM,
    STALE_HBM,
    TILES_HBM,
    WEIGHTS_HBM,
    COTANGENT_HBM,
    INDEX_HBM,
    COUNT_HBM,
}
IN_HBM = ARGS_HBM | {STATES_OUT}


def dot_f32(a, b):
    return jnp.dot(a, b, preferred_element_type=jnp.float32)


def dot_t(a, b):
    return lax.dot_general(a, b, (((0,), (0,)), ((), ())), preferred_element_type=jnp.float32)


class Plan:
    def __init__(self, tick, stream, sections, steps):
        self.tick = tick
        self.stream = stream
        self.sections = sections
        self.steps = steps
        self.last = tick == 2 * sections + 2 * steps - 3
        self.forward = tick <= sections - 1 + 2 * (steps - 1)
        self.backward = tick >= sections
        self.load_first = tick == 0 and stream == 0
        self.load_rest = tick == 0 and stream == STREAMS - 1
        self.first_mix = tick == 0 and PHASES[stream] == 0
        self.turn = stream == 0 and tick in (sections - 2, sections - 1)
        behind = (tick - 2 * sections) // 2
        self.weight = behind if (stream == STREAMS - 1 and 0 <= behind < steps - 1) else None
        self.flush = self.weight == 0
        reads, writes = set(), set()
        if self.load_first:
            reads |= {STALE_HBM, WEIGHTS_HBM}
            writes |= {STALE, WEIGHTS}
        if self.load_first or self.load_rest:
            reads |= {FEATURES_HBM, TILES_HBM}
            writes |= {FEATURES, TILES}
        if self.first_mix:
            reads |= {INDEX_HBM, COUNT_HBM, FEATURES, STALE, TILES}
            writes |= {MIX}
        if self.forward:
            reads |= {FEATURES, WEIGHTS, MIX}
            writes |= {SLOPE, ROUNDED, STATES}
        if self.turn:
            reads |= {WEIGHTS}
            writes |= {WEIGHTS_T}
        if self.backward:
            reads |= {COTANGENT, WEIGHTS_T, SLOPE}
            writes |= {SCALED, GRADS}
        if self.weight is not None:
            reads |= {ROUNDED, SCALED}
            writes |= {TOTAL}
        if self.flush:
            reads |= {STATES}
            writes |= {STATES_OUT}
        self.reads, self.writes = reads, writes


def compute_mix(ref, first, count, per_group):
    index, counts, placed = ref[INDEX_SMEM], ref[COUNT_SMEM], ref[PLACED]
    _, relations, _, slots, _, _ = ref[TILES].shape
    size = count * TILE
    placed[0:size, :] = jnp.zeros((size, placed.shape[1]), placed.dtype)
    for n in range(count):
        item, row = divmod(first + n, per_group)
        here = slice(n * TILE, (n + 1) * TILE)
        for r in range(relations):
            for k in range(slots):

                @pl.when(k < counts[item, r, row])
                def _():
                    cols = pl.ds(pl.multiple_of(index[item, r, k, row] * TILE, TILE), TILE)
                    placed[here, cols] = placed[here, cols] + ref[TILES][item, r, row, k]

    rows = slice(first * TILE, first * TILE + size)
    anchor = mix_alpha * ref[FEATURES][rows, :].astype(jnp.float32)
    for depth in range(ref[STALE].shape[0]):
        aggregate = dot_f32(placed[0:size, :], ref[STALE][depth])
        ref[MIX][depth, rows, :] = (1.0 - mix_alpha) * aggregate + anchor


def table_copies(ref, sems):
    return [
        pltpu.make_async_copy(ref[INDEX_HBM], ref[INDEX_SMEM], sems.at[0]),
        pltpu.make_async_copy(ref[COUNT_HBM], ref[COUNT_SMEM], sems.at[1]),
    ]


def beta_of(layer, layers):
    value = jnp.float32(math.log(theta_scale + 1.0))
    for n in range(1, layers):
        value = jnp.where(layer == n, jnp.float32(math.log(theta_scale / (n + 1) + 1.0)), value)
    return value


def forward_chunk(ref, rows, section, sections, recv, send):
    depths = ref[WEIGHTS].shape[0]
    anchor = ref[FEATURES][rows, :]
    send[...] = anchor if recv is None else jnp.where(section == 0, anchor, recv[...])

    @pl.loop(0, depths)
    def _(depth):
        half_beta = 0.5 * beta_of(section * depths + depth, sections * depths)
        hidden = send[...].astype(jnp.float32)
        mixed = (1.0 - mix_alpha) * hidden + ref[MIX][depth, rows, :]
        rounded = mixed.astype(jnp.bfloat16)
        ref[ROUNDED][depth, rows, :] = rounded
        z = (0.5 - half_beta) * mixed + half_beta * dot_f32(rounded, ref[WEIGHTS][depth])
        t = jnp.tanh(z)
        up = 1.0 + t
        silu = z * up
        ref[SLOPE][depth, rows, :] = (up + silu * (1.0 - t)).astype(jnp.bfloat16)
        send[...] = ((hidden + silu) * residual_scale).astype(jnp.bfloat16)

    ref[STATES][rows, :] = send[...]


def backward_chunk(ref, rows, section, sections, recv, send, carry):
    depths = ref[WEIGHTS_T].shape[0]
    last = ref[COTANGENT][rows, :]
    carry[...] = jnp.where(section == sections - 1, last, recv[...]).astype(jnp.float32)

    @pl.loop(0, depths)
    def _(step):
        depth = depths - 1 - step
        beta = beta_of(section * depths + depth, sections * depths)
        kept = residual_scale * carry[...]
        d_before = (0.5 * kept) * ref[SLOPE][depth, rows, :].astype(jnp.float32)
        d_scaled = (beta * d_before).astype(jnp.bfloat16)
        ref[SCALED][depth, rows, :] = d_scaled
        product = dot_f32(d_scaled, ref[WEIGHTS_T][depth])
        direct = kept + ((1.0 - mix_alpha) * (1.0 - beta)) * d_before
        carry[...] = direct + (1.0 - mix_alpha) * product

    grad = carry[...].astype(jnp.bfloat16)
    ref[GRADS][rows, :] = grad
    if send is not None:
        send[...] = grad


def extra_kernel(sections, steps, per_group, names_in, names_out, *refs):
    refs = list(refs)
    ref = {name: refs.pop(0) for name in names_in}
    ref.update({name: refs.pop(0) for name in names_out})
    ref[INDEX_SMEM], ref[COUNT_SMEM], ref[PLACED], sems = refs
    last = lax.axis_index("section") == sections - 1
    tables = table_copies(ref, sems)
    cotangent = pltpu.make_async_copy(ref[COTANGENT_HBM], ref[COTANGENT], sems.at[2])
    for copy in tables:
        copy.start()

    @pl.when(last)
    def _():
        cotangent.start()

    for copy in tables:
        copy.wait()
    for stream in range(STREAMS):
        if PHASES[stream]:
            compute_mix(ref, stream, 1, per_group)
    for step in range(1, steps):
        compute_mix(ref, step * STREAMS, STREAMS, per_group)

    @pl.when(last)
    def _():
        cotangent.wait()


def tick_kernel(plan, depths, per_group, names_in, names_out, *refs):
    refs = list(refs)
    recv = refs.pop(0) if plan.tick else None
    ref = {name: refs.pop(0) for name in names_in}
    send = None if plan.last else refs.pop(0)
    ref.update({name: refs.pop(0) for name in names_out})
    carry = refs.pop(0) if plan.backward else None
    if plan.first_mix:
        ref[INDEX_SMEM], ref[COUNT_SMEM], ref[PLACED] = refs.pop(0), refs.pop(0), refs.pop(0)
    sems = refs.pop(0) if refs else None
    section = lax.axis_index("section")
    sections, tick, stream = plan.sections, plan.tick, plan.stream
    own = lax.rem(section + tick, 2) == 0

    if plan.first_mix:
        tables = table_copies(ref, sems)
        for copy in tables:
            copy.start()
    group = per_group * TILE
    rest = []
    if plan.load_rest:
        items = ref[TILES].shape[0]
        spare, others = pl.ds(group, (items - 1) * group), pl.ds(1, items - 1)
        rest = [
            pltpu.make_async_copy(ref[TILES_HBM].at[others], ref[TILES].at[others], sems.at[2]),
            pltpu.make_async_copy(ref[FEATURES_HBM].at[spare], ref[FEATURES].at[spare], sems.at[3]),
        ]
        for copy in rest:
            copy.start()
    if plan.load_first:
        item = pl.ds(0, group)
        first = [
            pltpu.make_async_copy(ref[TILES_HBM].at[0], ref[TILES].at[0], sems.at[2]),
            pltpu.make_async_copy(ref[STALE_HBM], ref[STALE], sems.at[3]),
            pltpu.make_async_copy(ref[FEATURES_HBM].at[item], ref[FEATURES].at[item], sems.at[4]),
            pltpu.make_async_copy(ref[WEIGHTS_HBM], ref[WEIGHTS], sems.at[5]),
        ]
        for copy in first:
            copy.start()
        for copy in first[:3]:
            copy.wait()
    if plan.first_mix:
        for copy in tables:
            copy.wait()
        compute_mix(ref, stream, 1, per_group)
    if plan.load_first:
        first[3].wait()

    def rows_of(step):
        return pl.ds(pl.multiple_of((step * STREAMS + stream) * TILE, TILE), TILE)

    if plan.forward:
        twice = tick - section

        @pl.when(own & (twice >= 0) & (twice < 2 * plan.steps))
        def _():
            forward_chunk(ref, rows_of(lax.div(twice, 2)), section, sections, recv, send)

    if plan.turn:

        @pl.when(jnp.logical_not(own))
        def _():
            side = 2 * TILE
            blocks = ref[WEIGHTS].shape[1] // side

            @pl.loop(0, depths * blocks * blocks)
            def _(n):
                depth = lax.div(n, blocks * blocks)
                down = pl.ds(pl.multiple_of(lax.rem(lax.div(n, blocks), blocks) * side, side), side)
                along = pl.ds(pl.multiple_of(lax.rem(n, blocks) * side, side), side)
                ref[WEIGHTS_T][depth, along, down] = ref[WEIGHTS][depth, down, along].T

    if plan.backward:
        twice_back = tick - (2 * sections - 1) + section

        @pl.when(jnp.logical_not(own) & (twice_back >= 0) & (twice_back < 2 * plan.steps))
        def _():
            rows = rows_of(lax.div(twice_back, 2))
            backward_chunk(ref, rows, section, sections, recv, send, carry)

    if plan.weight is not None:
        size = STREAMS * TILE
        rows = slice(plan.weight * size, (plan.weight + 1) * size)

        @pl.when(own)
        def _():
            if plan.flush:
                copy = pltpu.make_async_copy(ref[STATES], ref[STATES_OUT], sems.at[0])
                copy.start()

            @pl.loop(0, depths)
            def _(depth):
                term = dot_t(ref[ROUNDED][depth, rows, :], ref[SCALED][depth, rows, :])
                if plan.weight == 0:
                    ref[TOTAL][depth] = term
                else:
                    ref[TOTAL][depth] += term

            if plan.flush:
                copy.wait()

    for copy in rest:
        copy.wait()


def finish_kernel(rows, reps, rounded, scaled, total, grads, keep, give, grads_out, sem):
    copy = pltpu.make_async_copy(grads, grads_out, sem)
    copy.start()
    depths, width, _ = total.shape
    share = width // reps
    core = lax.rem(lax.axis_index("rep"), 2)

    @pl.loop(0, depths)
    def _(depth):
        term = dot_t(rounded[depth, rows, :], scaled[depth, rows, :])
        full = ((total[depth] + term) * (1.0 / reps)).astype(jnp.bfloat16)
        for q in range(reps // 2):
            even = full[2 * q * share : (2 * q + 1) * share, :]
            odd = full[(2 * q + 1) * share : (2 * q + 2) * share, :]
            place = pl.ds(pl.multiple_of((q * depths + depth) * share, share), share)
            keep[place, :] = jnp.where(core == 0, even, odd)
            give[place, :] = jnp.where(core == 0, odd, even)

    copy.wait()


def spec_of(name):
    space = pltpu.HBM if name in IN_HBM else pltpu.VMEM
    return pl.BlockSpec(memory_space=space)


def body(features, stale_states, tile_values, tile_index, tile_count, weights, cotangent):
    sections = lax.axis_size("section")
    reps = lax.axis_size("rep")
    depths = weights.shape[0]
    nodes, width = features.shape
    per_group = tile_values.shape[2]
    steps = nodes // (STREAMS * TILE)
    ticks = 2 * sections - 2 + 2 * steps

    buffers = {
        FEATURES_HBM: features,
        STALE_HBM: stale_states,
        TILES_HBM: tile_values,
        WEIGHTS_HBM: weights,
        COTANGENT_HBM: cotangent,
        INDEX_HBM: jnp.swapaxes(tile_index, 2, 3),
        COUNT_HBM: tile_count,
    }
    low, wide = jnp.bfloat16, jnp.float32
    struct = jax.ShapeDtypeStruct
    shapes = {
        FEATURES: struct(features.shape, low),
        STALE: struct(stale_states.shape, low),
        TILES: struct(tile_values.shape, low),
        WEIGHTS: struct(weights.shape, low),
        WEIGHTS_T: struct(weights.shape, low),
        COTANGENT: struct(cotangent.shape, low),
        MIX: struct((depths, nodes, width), wide),
        SLOPE: struct((depths, nodes, width), low),
        ROUNDED: struct((depths, nodes, width), low),
        SCALED: struct((depths, nodes, width), low),
        STATES: struct((nodes, width), low),
        STATES_OUT: struct((nodes, width), low),
        GRADS: struct((nodes, width), low),
        TOTAL: struct((depths, width, width), wide),
    }
    parcel = struct((TILE, width), low)
    exchange = [
        [(i, i ^ 1) for i in range(sections)],
        [((i + 1) % sections, ((i ^ 1) + 1) % sections) for i in range(sections)],
    ]
    tables = [pltpu.SMEM(buffers[n].shape, jnp.int32) for n in (INDEX_HBM, COUNT_HBM)]
    tables.append(pltpu.VMEM((STREAMS * TILE, stale_states.shape[1]), low))

    def call(kernel, name, reads, writes, mail_in, mail_out, scratch):
        names_out = sorted(writes)
        names_in = sorted((reads | writes) & set(buffers))
        operands = [
            pltpu.with_memory_space_constraint(buffers[n], pltpu.HBM) if n in ARGS_HBM else buffers[n]
            for n in names_in
        ]
        results = pl.pallas_call(
            functools.partial(kernel, names_in, names_out),
            out_shape=mail_out + [shapes[n] for n in names_out],
            in_specs=[spec_of(None) for _ in mail_in] + [spec_of(n) for n in names_in],
            out_specs=[spec_of(None) for _ in mail_out] + [spec_of(n) for n in names_out],
            scratch_shapes=scratch,
            input_output_aliases={
                len(mail_in) + names_in.index(n): len(mail_out) + names_out.index(n)
                for n in names_out
                if n in buffers
            },
            compiler_params=pltpu.CompilerParams(vmem_limit_bytes=GRANT),
            cost_estimate=pl.CostEstimate(
                flops=4 * TILE * width * width, bytes_accessed=1 << 20, transcendentals=0
            ),
            name=name,
        )(*mail_in, *operands)
        buffers.update(zip(names_out, results[len(mail_out) :]))
        return results[: len(mail_out)]

    received = [None] * STREAMS
    for slot in range(ticks + max(PHASES)):
        for stream, phase in enumerate(PHASES):
            tick = slot - phase
            if not 0 <= tick < ticks:
                continue
            plan = Plan(tick, stream, sections, steps)
            mail_in = [received[stream]] if tick else []
            mail_out = [] if plan.last else [parcel]
            scratch = [pltpu.VMEM((TILE, width), wide)] if plan.backward else []
            if plan.first_mix:
                scratch += tables
            if plan.first_mix or plan.flush:
                scratch.append(pltpu.SemaphoreType.DMA((6,)))
            sent = call(
                functools.partial(tick_kernel, plan, depths, per_group),
                f"tick{tick}_{stream}",
                plan.reads,
                plan.writes,
                mail_in,
                mail_out,
                scratch,
            )
            if not plan.last:
                received[stream] = lax.ppermute(sent[0], "section", exchange[tick % 2])
        if slot == 0:
            call(
                functools.partial(extra_kernel, sections, steps, per_group),
                "mix",
                {INDEX_HBM, COUNT_HBM, FEATURES, STALE, TILES, COTANGENT_HBM},
                {MIX, STATES, COTANGENT},
                [],
                [],
                tables + [pltpu.SemaphoreType.DMA((3,))],
            )

    size = STREAMS * TILE
    half = struct((depths * width // 2, width), low)
    keep, give, grads_out = pl.pallas_call(
        functools.partial(finish_kernel, slice((steps - 1) * size, steps * size), reps),
        out_shape=[half, half, shapes[GRADS]],
        in_specs=[spec_of(None)] * 4,
        out_specs=[spec_of(None)] * 2 + [pl.BlockSpec(memory_space=pltpu.HBM)],
        scratch_shapes=[pltpu.SemaphoreType.DMA],
        compiler_params=pltpu.CompilerParams(vmem_limit_bytes=GRANT),
        name="finish",
    )(buffers[ROUNDED], buffers[SCALED], buffers[TOTAL], buffers[GRADS])
    got = lax.ppermute(give, "rep", [(i, i ^ 1) for i in range(reps)])
    chip = (keep.astype(wide) + got.astype(wide)).astype(low)
    parts = lax.all_to_all(
        chip.reshape(reps // 2, -1, width),
        "rep",
        split_axis=0,
        concat_axis=0,
        tiled=True,
        axis_index_groups=[list(range(core, reps, 2)) for core in range(2)],
    )
    weight_grads = parts.astype(wide).sum(0)
    return (
        buffers[STATES_OUT][None],
        grads_out[None],
        weight_grads.reshape(depths, width // reps, width),
    )


def solution(mesh):
    return jax.shard_map(
        body,
        mesh=mesh,
        in_specs=(
            P("rep", None),
            P("section", "rep", None),
            P("rep", None, None, None, None, None),
            P("rep", None, None, None),
            P("rep", None, None),
            P("section", None, None),
            P("rep", None),
        ),
        out_specs=(P("section", "rep", None), P("section", "rep", None), P("section", "rep", None)),
        check_vma=False,
    )
```

```python
import functools
import math

import jax
import jax.numpy as jnp
from jax import lax
from jax.experimental import pallas as pl
from jax.experimental.pallas import tpu as pltpu
from jax.sharding import PartitionSpec as P

TILE = 128
PHASES = (0, 1, 0)
STREAMS = len(PHASES)
GRANT = 8 << 20

mix_alpha = 0.1
theta_scale = 0.5
residual_scale = 0.5**0.5


(
    FEATURES_HBM,
    STALE_HBM,
    TILES_HBM,
    WEIGHTS_HBM,
    COTANGENT_HBM,
    INDEX_HBM,
    COUNT_HBM,
    FEATURES,
    STALE,
    TILES,
    WEIGHTS,
    WEIGHTS_T,
    COTANGENT,
    MIX,
    SLOPE,
    ROUNDED,
    SCALED,
    STATES,
    STATES_OUT,
    GRADS,
    TOTAL,
    INDEX_SMEM,
    COUNT_SMEM,
    PLACED,
) = range(24)

ARGS_HBM = {
    FEATURES_HBM,
    STALE_HBM,
    TILES_HBM,
    WEIGHTS_HBM,
    COTANGENT_HBM,
    INDEX_HBM,
    COUNT_HBM,
}
IN_HBM = ARGS_HBM | {STATES_OUT}


def dot_f32(a, b):
    return jnp.dot(a, b, preferred_element_type=jnp.float32)


def dot_t(a, b):
    return lax.dot_general(a, b, (((0,), (0,)), ((), ())), preferred_element_type=jnp.float32)


class Plan:
    def __init__(self, tick, stream, sections, steps):
        self.tick = tick
        self.stream = stream
        self.sections = sections
        self.steps = steps
        self.last = tick == 2 * sections + 2 * steps - 3
        self.forward = tick <= sections - 1 + 2 * (steps - 1)
        self.backward = tick >= sections
        self.load_first = tick == 0 and stream == 0
        self.load_rest = tick == 0 and stream == STREAMS - 1
        self.first_mix = tick == 0 and PHASES[stream] == 0
        reads, writes = set(), set()
        if self.load_first:
            reads |= {STALE_HBM, WEIGHTS_HBM}
            writes |= {STALE, WEIGHTS}
        if self.load_first or self.load_rest:
            reads |= {FEATURES_HBM, TILES_HBM}
            writes |= {FEATURES, TILES}
        if self.first_mix:
            reads |= {INDEX_HBM, COUNT_HBM, FEATURES, STALE, TILES}
            writes |= {MIX}
        if self.forward:
            reads |= {FEATURES, WEIGHTS, MIX}
            writes |= {SLOPE, ROUNDED, STATES}
        if self.backward:
            reads |= {COTANGENT, WEIGHTS_T, SLOPE}
            writes |= {SCALED, GRADS}
        self.reads, self.writes = reads, writes


def compute_mix(ref, first, count, per_group):
    index, counts, placed = ref[INDEX_SMEM], ref[COUNT_SMEM], ref[PLACED]
    _, relations, _, slots, _, _ = ref[TILES].shape
    size = count * TILE
    placed[0:size, :] = jnp.zeros((size, placed.shape[1]), placed.dtype)
    for n in range(count):
        item, row = divmod(first + n, per_group)
        here = slice(n * TILE, (n + 1) * TILE)
        for r in range(relations):
            for k in range(slots):

                @pl.when(k < counts[item, r, row])
                def _():
                    cols = pl.ds(pl.multiple_of(index[item, r, k, row] * TILE, TILE), TILE)
                    placed[here, cols] = placed[here, cols] + ref[TILES][item, r, row, k]

    rows = slice(first * TILE, first * TILE + size)
    anchor = mix_alpha * ref[FEATURES][rows, :].astype(jnp.float32)
    for depth in range(ref[STALE].shape[0]):
        aggregate = dot_f32(placed[0:size, :], ref[STALE][depth])
        ref[MIX][depth, rows, :] = (1.0 - mix_alpha) * aggregate + anchor


def table_copies(ref, sems):
    return [
        pltpu.make_async_copy(ref[INDEX_HBM], ref[INDEX_SMEM], sems.at[0]),
        pltpu.make_async_copy(ref[COUNT_HBM], ref[COUNT_SMEM], sems.at[1]),
    ]


def beta_of(layer, layers):
    value = jnp.float32(math.log(theta_scale + 1.0))
    for n in range(1, layers):
        value = jnp.where(layer == n, jnp.float32(math.log(theta_scale / (n + 1) + 1.0)), value)
    return value


def forward_chunk(ref, rows, section, sections, recv, send):
    depths = ref[WEIGHTS].shape[0]
    current = ref[FEATURES][rows, :]
    if recv is not None:
        current = jnp.where(section == 0, current, recv[...])
    for depth in range(depths):
        half_beta = 0.5 * beta_of(section * depths + depth, sections * depths)
        hidden = current.astype(jnp.float32)
        mixed = (1.0 - mix_alpha) * hidden + ref[MIX][depth, rows, :]
        rounded = mixed.astype(jnp.bfloat16)
        ref[ROUNDED][depth, rows, :] = rounded
        z = (0.5 - half_beta) * mixed + half_beta * dot_f32(rounded, ref[WEIGHTS][depth])
        t = jnp.tanh(z)
        up = 1.0 + t
        silu = z * up
        ref[SLOPE][depth, rows, :] = (up + silu * (1.0 - t)).astype(jnp.bfloat16)
        current = ((hidden + silu) * residual_scale).astype(jnp.bfloat16)
    send[...] = current
    ref[STATES][rows, :] = current


def backward_chunk(ref, rows, section, sections, recv, send):
    depths = ref[WEIGHTS_T].shape[0]
    last = ref[COTANGENT][rows, :]
    upstream = jnp.where(section == sections - 1, last, recv[...]).astype(jnp.float32)
    for depth in reversed(range(depths)):
        beta = beta_of(section * depths + depth, sections * depths)
        kept = residual_scale * upstream
        d_before = (0.5 * kept) * ref[SLOPE][depth, rows, :].astype(jnp.float32)
        d_scaled = (beta * d_before).astype(jnp.bfloat16)
        ref[SCALED][depth, rows, :] = d_scaled
        product = dot_f32(d_scaled, ref[WEIGHTS_T][depth])
        direct = kept + ((1.0 - mix_alpha) * (1.0 - beta)) * d_before
        upstream = direct + (1.0 - mix_alpha) * product
    grad = upstream.astype(jnp.bfloat16)
    if send is not None:
        send[...] = grad
    ref[GRADS][rows, :] = grad


def extra_kernel(slot, sections, steps, per_group, names_in, names_out, *refs):
    refs = list(refs)
    ref = {name: refs.pop(0) for name in names_in}
    ref.update({name: refs.pop(0) for name in names_out})
    ref[INDEX_SMEM], ref[COUNT_SMEM], ref[PLACED], sems = refs
    section = lax.axis_index("section")
    tables = table_copies(ref, sems)
    if slot == 0:
        for copy in tables:
            copy.start()
        for copy in tables:
            copy.wait()
        for stream in range(STREAMS):
            if PHASES[stream]:
                compute_mix(ref, stream, 1, per_group)
        compute_mix(ref, STREAMS, STREAMS, per_group)
        return

    @pl.when(lax.rem(section + slot, 2) == 1)
    def _():
        for copy in tables:
            copy.start()
        if slot == 2:
            cotangent = pltpu.make_async_copy(ref[COTANGENT_HBM], ref[COTANGENT], sems.at[2])

            @pl.when(section == sections - 1)
            def _():
                cotangent.start()

        for copy in tables:
            copy.wait()
        for step in range(2, steps):
            compute_mix(ref, step * STREAMS, STREAMS, per_group)
        if slot == 2:

            @pl.when(section == sections - 1)
            def _():
                cotangent.wait()


def turn_kernel(slot, names_in, names_out, *refs):
    ref = dict(zip(names_in + names_out, refs))

    @pl.when(lax.rem(lax.axis_index("section") + slot, 2) == 1)
    def _():
        depths, width, _ = ref[WEIGHTS].shape
        side = 2 * TILE
        blocks = width // side

        @pl.loop(0, depths * blocks * blocks)
        def _(n):
            depth = lax.div(n, blocks * blocks)
            down = pl.ds(pl.multiple_of(lax.rem(lax.div(n, blocks), blocks) * side, side), side)
            along = pl.ds(pl.multiple_of(lax.rem(n, blocks) * side, side), side)
            ref[WEIGHTS_T][depth, along, down] = ref[WEIGHTS][depth, down, along].T


def weight_kernel(slot, step, names_in, names_out, *refs):
    ref = dict(zip(names_in + names_out, refs))
    size = STREAMS * TILE
    rows = slice(step * size, (step + 1) * size)

    @pl.when(lax.rem(lax.axis_index("section") + slot, 2) == 0)
    def _():
        if step == 0:
            copy = pltpu.make_async_copy(ref[STATES], ref[STATES_OUT], refs[-1])
            copy.start()

        @pl.loop(0, ref[TOTAL].shape[0])
        def _(depth):
            term = dot_t(ref[ROUNDED][depth, rows, :], ref[SCALED][depth, rows, :])
            if step == 0:
                ref[TOTAL][depth] = term
            else:
                ref[TOTAL][depth] += term

        if step == 0:
            copy.wait()


def tick_kernel(plan, depths, per_group, names_in, names_out, *refs):
    refs = list(refs)
    recv = refs.pop(0) if plan.tick else None
    ref = {name: refs.pop(0) for name in names_in}
    send = None if plan.last else refs.pop(0)
    ref.update({name: refs.pop(0) for name in names_out})
    if plan.first_mix:
        ref[INDEX_SMEM], ref[COUNT_SMEM], ref[PLACED] = refs.pop(0), refs.pop(0), refs.pop(0)
    sems = refs.pop(0) if refs else None
    section = lax.axis_index("section")
    sections, tick, stream = plan.sections, plan.tick, plan.stream
    own = lax.rem(section + tick, 2) == 0

    if plan.first_mix:
        tables = table_copies(ref, sems)
        for copy in tables:
            copy.start()
    group = per_group * TILE
    rest = []
    if plan.load_rest:
        items = ref[TILES].shape[0]
        spare, others = pl.ds(group, (items - 1) * group), pl.ds(1, items - 1)
        rest = [
            pltpu.make_async_copy(ref[TILES_HBM].at[others], ref[TILES].at[others], sems.at[2]),
            pltpu.make_async_copy(ref[FEATURES_HBM].at[spare], ref[FEATURES].at[spare], sems.at[3]),
        ]
        for copy in rest:
            copy.start()
    if plan.load_first:
        item = pl.ds(0, group)
        first = [
            pltpu.make_async_copy(ref[TILES_HBM].at[0], ref[TILES].at[0], sems.at[2]),
            pltpu.make_async_copy(ref[STALE_HBM], ref[STALE], sems.at[3]),
            pltpu.make_async_copy(ref[FEATURES_HBM].at[item], ref[FEATURES].at[item], sems.at[4]),
            pltpu.make_async_copy(ref[WEIGHTS_HBM], ref[WEIGHTS], sems.at[5]),
        ]
        for copy in first:
            copy.start()
        for copy in first[:3]:
            copy.wait()
    if plan.first_mix:
        for copy in tables:
            copy.wait()
        compute_mix(ref, stream, 1, per_group)
    if plan.load_first:
        first[3].wait()

    def rows_of(step):
        return pl.ds(pl.multiple_of((step * STREAMS + stream) * TILE, TILE), TILE)

    if plan.forward:
        twice = tick - section

        @pl.when(own & (twice >= 0) & (twice < 2 * plan.steps))
        def _():
            forward_chunk(ref, rows_of(lax.div(twice, 2)), section, sections, recv, send)

    if plan.backward:
        twice_back = tick - (2 * sections - 1) + section

        @pl.when(jnp.logical_not(own) & (twice_back >= 0) & (twice_back < 2 * plan.steps))
        def _():
            rows = rows_of(lax.div(twice_back, 2))
            backward_chunk(ref, rows, section, sections, recv, send)

    for copy in rest:
        copy.wait()


def finish_kernel(rows, reps, rounded, scaled, total, grads, keep, give, grads_out, sem):
    copy = pltpu.make_async_copy(grads, grads_out, sem)
    copy.start()
    depths, width, _ = total.shape
    share = width // reps
    core = lax.rem(lax.axis_index("rep"), 2)

    @pl.loop(0, depths)
    def _(depth):
        term = dot_t(rounded[depth, rows, :], scaled[depth, rows, :])
        full = ((total[depth] + term) * (1.0 / reps)).astype(jnp.bfloat16)
        for q in range(reps // 2):
            even = full[2 * q * share : (2 * q + 1) * share, :]
            odd = full[(2 * q + 1) * share : (2 * q + 2) * share, :]
            place = pl.ds(pl.multiple_of((q * depths + depth) * share, share), share)
            keep[place, :] = jnp.where(core == 0, even, odd)
            give[place, :] = jnp.where(core == 0, odd, even)

    copy.wait()


def spec_of(name):
    space = pltpu.HBM if name in IN_HBM else pltpu.VMEM
    return pl.BlockSpec(memory_space=space)


def body(features, stale_states, tile_values, tile_index, tile_count, weights, cotangent):
    sections = lax.axis_size("section")
    reps = lax.axis_size("rep")
    depths = weights.shape[0]
    nodes, width = features.shape
    per_group = tile_values.shape[2]
    steps = nodes // (STREAMS * TILE)
    ticks = 2 * sections - 2 + 2 * steps

    buffers = {
        FEATURES_HBM: features,
        STALE_HBM: stale_states,
        TILES_HBM: tile_values,
        WEIGHTS_HBM: weights,
        COTANGENT_HBM: cotangent,
        INDEX_HBM: jnp.swapaxes(tile_index, 2, 3),
        COUNT_HBM: tile_count,
    }
    low, wide = jnp.bfloat16, jnp.float32
    struct = jax.ShapeDtypeStruct
    shapes = {
        FEATURES: struct(features.shape, low),
        STALE: struct(stale_states.shape, low),
        TILES: struct(tile_values.shape, low),
        WEIGHTS: struct(weights.shape, low),
        WEIGHTS_T: struct(weights.shape, low),
        COTANGENT: struct(cotangent.shape, low),
        MIX: struct((depths, nodes, width), wide),
        SLOPE: struct((depths, nodes, width), low),
        ROUNDED: struct((depths, nodes, width), low),
        SCALED: struct((depths, nodes, width), low),
        STATES: struct((nodes, width), low),
        STATES_OUT: struct((nodes, width), low),
        GRADS: struct((nodes, width), low),
        TOTAL: struct((depths, width, width), wide),
    }
    parcel = struct((TILE, width), low)
    exchange = [
        [(i, i ^ 1) for i in range(sections)],
        [((i + 1) % sections, ((i ^ 1) + 1) % sections) for i in range(sections)],
    ]
    tables = [pltpu.SMEM(buffers[n].shape, jnp.int32) for n in (INDEX_HBM, COUNT_HBM)]
    tables.append(pltpu.VMEM((STREAMS * TILE, stale_states.shape[1]), low))

    def call(kernel, name, reads, writes, mail_in, mail_out, scratch):
        names_out = sorted(writes)
        names_in = sorted((reads | writes) & set(buffers))
        operands = [
            pltpu.with_memory_space_constraint(buffers[n], pltpu.HBM) if n in ARGS_HBM else buffers[n]
            for n in names_in
        ]
        results = pl.pallas_call(
            functools.partial(kernel, names_in, names_out),
            out_shape=mail_out + [shapes[n] for n in names_out],
            in_specs=[spec_of(None) for _ in mail_in] + [spec_of(n) for n in names_in],
            out_specs=[spec_of(None) for _ in mail_out] + [spec_of(n) for n in names_out],
            scratch_shapes=scratch,
            input_output_aliases={
                len(mail_in) + names_in.index(n): len(mail_out) + names_out.index(n)
                for n in names_out
                if n in buffers
            },
            compiler_params=pltpu.CompilerParams(vmem_limit_bytes=GRANT),
            cost_estimate=pl.CostEstimate(
                flops=4 * TILE * width * width, bytes_accessed=1 << 20, transcendentals=0
            ),
            name=name,
        )(*mail_in, *operands)
        buffers.update(zip(names_out, results[len(mail_out) :]))
        return results[: len(mail_out)]

    received = [None] * STREAMS
    for slot in range(ticks + max(PHASES)):
        for stream, phase in enumerate(PHASES):
            tick = slot - phase
            if not 0 <= tick < ticks:
                continue
            plan = Plan(tick, stream, sections, steps)
            mail_in = [received[stream]] if tick else []
            mail_out = [] if plan.last else [parcel]
            scratch = list(tables) if plan.first_mix else []
            if plan.first_mix:
                scratch.append(pltpu.SemaphoreType.DMA((6,)))
            sent = call(
                functools.partial(tick_kernel, plan, depths, per_group),
                f"tick{tick}_{stream}",
                plan.reads,
                plan.writes,
                mail_in,
                mail_out,
                scratch,
            )
            if not plan.last:
                received[stream] = lax.ppermute(sent[0], "section", exchange[tick % 2])
        if slot < 3:
            call(
                functools.partial(extra_kernel, slot, sections, steps, per_group),
                f"mix{slot}",
                {INDEX_HBM, COUNT_HBM, FEATURES, STALE, TILES} | ({COTANGENT_HBM} if slot == 2 else set()),
                {MIX, STATES} | ({COTANGENT} if slot == 2 else set()),
                [],
                [],
                tables + [pltpu.SemaphoreType.DMA((3,))],
            )
        if slot in (3, 4):
            call(
                functools.partial(turn_kernel, slot), f"turn{slot}", {WEIGHTS}, {WEIGHTS_T, STATES}, [], [], []
            )
        step = (slot - 2 * sections) // 2
        if 0 <= step < steps - 1:
            call(
                functools.partial(weight_kernel, slot, step),
                f"weight{slot}",
                {ROUNDED, STATES} if step == 0 else {ROUNDED},
                {TOTAL, SCALED, GRADS} | ({STATES_OUT} if step == 0 else set()),
                [],
                [],
                [pltpu.SemaphoreType.DMA] if step == 0 else [],
            )

    size = STREAMS * TILE
    half = struct((depths * width // 2, width), low)
    keep, give, grads_out = pl.pallas_call(
        functools.partial(finish_kernel, slice((steps - 1) * size, steps * size), reps),
        out_shape=[half, half, shapes[GRADS]],
        in_specs=[spec_of(None)] * 4,
        out_specs=[spec_of(None)] * 2 + [pl.BlockSpec(memory_space=pltpu.HBM)],
        scratch_shapes=[pltpu.SemaphoreType.DMA],
        compiler_params=pltpu.CompilerParams(vmem_limit_bytes=GRANT),
        name="finish",
    )(buffers[ROUNDED], buffers[SCALED], buffers[TOTAL], buffers[GRADS])
    got = lax.ppermute(give, "rep", [(i, i ^ 1) for i in range(reps)])
    chip = (keep.astype(wide) + got.astype(wide)).astype(low)
    parts = lax.all_to_all(
        chip.reshape(reps // 2, -1, width),
        "rep",
        split_axis=0,
        concat_axis=0,
        tiled=True,
        axis_index_groups=[list(range(core, reps, 2)) for core in range(2)],
    )
    weight_grads = parts.astype(wide).sum(0)
    return (
        buffers[STATES_OUT][None],
        grads_out[None],
        weight_grads.reshape(depths, width // reps, width),
    )


def solution(mesh):
    return jax.shard_map(
        body,
        mesh=mesh,
        in_specs=(
            P("rep", None),
            P("section", "rep", None),
            P("rep", None, None, None, None, None),
            P("rep", None, None, None),
            P("rep", None, None),
            P("section", None, None),
            P("rep", None),
        ),
        out_specs=(P("section", "rep", None), P("section", "rep", None), P("section", "rep", None)),
        check_vma=False,
    )
```

```python
import functools
import math

import jax
import jax.numpy as jnp
from jax import lax
from jax.experimental import pallas as pl
from jax.experimental.pallas import tpu as pltpu
from jax.sharding import PartitionSpec as P

TILE = 128
PHASES = (0, 1, 0)
STREAMS = len(PHASES)
GRANT = 8 << 20

mix_alpha = 0.1
theta_scale = 0.5
residual_scale = 0.5**0.5


(
    FEATURES_HBM,
    STALE_HBM,
    TILES_HBM,
    WEIGHTS_HBM,
    COTANGENT_HBM,
    INDEX_HBM,
    COUNT_HBM,
    FEATURES,
    STALE,
    TILES,
    WEIGHTS,
    WEIGHTS_T,
    COTANGENT,
    MIX,
    SLOPE,
    ROUNDED,
    SCALED,
    STATES,
    STATES_OUT,
    GRADS,
    TOTAL,
    INDEX_SMEM,
    COUNT_SMEM,
    PLACED,
) = range(24)

ARGS_HBM = {
    FEATURES_HBM,
    STALE_HBM,
    TILES_HBM,
    WEIGHTS_HBM,
    COTANGENT_HBM,
    INDEX_HBM,
    COUNT_HBM,
}
IN_HBM = ARGS_HBM | {STATES_OUT}


def dot_f32(a, b):
    return jnp.dot(a, b, preferred_element_type=jnp.float32)


def dot_t(a, b):
    return lax.dot_general(a, b, (((0,), (0,)), ((), ())), preferred_element_type=jnp.float32)


class Plan:
    def __init__(self, tick, stream, sections, steps):
        self.tick = tick
        self.stream = stream
        self.sections = sections
        self.steps = steps
        self.last = tick == 2 * sections + 2 * steps - 3
        self.forward = tick <= sections - 1 + 2 * (steps - 1)
        self.backward = tick >= sections
        self.load_first = tick == 0 and stream == 0
        self.load_rest = tick == 0 and stream == STREAMS - 1
        self.first_mix = tick == 0 and PHASES[stream] == 0
        reads, writes = set(), set()
        if self.load_first:
            reads |= {STALE_HBM, WEIGHTS_HBM}
            writes |= {STALE, WEIGHTS}
        if self.load_first or self.load_rest:
            reads |= {FEATURES_HBM, TILES_HBM}
            writes |= {FEATURES, TILES}
        if self.first_mix:
            reads |= {INDEX_HBM, COUNT_HBM, FEATURES, STALE, TILES}
            writes |= {MIX}
        if self.forward:
            reads |= {FEATURES, WEIGHTS, MIX}
            writes |= {SLOPE, ROUNDED, STATES}
        if self.backward:
            reads |= {COTANGENT, WEIGHTS_T, SLOPE}
            writes |= {SCALED, GRADS}
        self.reads, self.writes = reads, writes


def compute_mix(ref, first, count, per_group):
    index, counts, placed = ref[INDEX_SMEM], ref[COUNT_SMEM], ref[PLACED]
    _, relations, _, slots, _, _ = ref[TILES].shape
    size = count * TILE
    placed[0:size, :] = jnp.zeros((size, placed.shape[1]), placed.dtype)
    for n in range(count):
        item, row = divmod(first + n, per_group)
        here = slice(n * TILE, (n + 1) * TILE)
        for r in range(relations):
            for k in range(slots):

                @pl.when(k < counts[item, r, row])
                def _():
                    cols = pl.ds(pl.multiple_of(index[item, r, k, row] * TILE, TILE), TILE)
                    placed[here, cols] = placed[here, cols] + ref[TILES][item, r, row, k]

    rows = slice(first * TILE, first * TILE + size)
    anchor = mix_alpha * ref[FEATURES][rows, :].astype(jnp.float32)
    for depth in range(ref[STALE].shape[0]):
        aggregate = dot_f32(placed[0:size, :], ref[STALE][depth])
        ref[MIX][depth, rows, :] = (1.0 - mix_alpha) * aggregate + anchor


def table_copies(ref, sems):
    return [
        pltpu.make_async_copy(ref[INDEX_HBM], ref[INDEX_SMEM], sems.at[0]),
        pltpu.make_async_copy(ref[COUNT_HBM], ref[COUNT_SMEM], sems.at[1]),
    ]


def beta_of(layer, layers):
    value = jnp.float32(math.log(theta_scale + 1.0))
    for n in range(1, layers):
        value = jnp.where(layer == n, jnp.float32(math.log(theta_scale / (n + 1) + 1.0)), value)
    return value


def forward_chunk(ref, rows, section, sections, recv, send):
    depths = ref[WEIGHTS].shape[0]
    current = ref[FEATURES][rows, :]
    if recv is not None:
        current = jnp.where(section == 0, current, recv[...])
    for depth in range(depths):
        half_beta = 0.5 * beta_of(section * depths + depth, sections * depths)
        hidden = current.astype(jnp.float32)
        mixed = (1.0 - mix_alpha) * hidden + ref[MIX][depth, rows, :]
        rounded = mixed.astype(jnp.bfloat16)
        ref[ROUNDED][depth, rows, :] = rounded
        z = (0.5 - half_beta) * mixed + half_beta * dot_f32(rounded, ref[WEIGHTS][depth])
        t = jnp.tanh(z)
        up = 1.0 + t
        silu = z * up
        ref[SLOPE][depth, rows, :] = (up + silu * (1.0 - t)).astype(jnp.bfloat16)
        current = ((hidden + silu) * residual_scale).astype(jnp.bfloat16)
    send[...] = current
    ref[STATES][rows, :] = current


def backward_chunk(ref, rows, section, sections, recv, send):
    depths = ref[WEIGHTS_T].shape[0]
    last = ref[COTANGENT][rows, :]
    upstream = jnp.where(section == sections - 1, last, recv[...]).astype(jnp.float32)
    for depth in reversed(range(depths)):
        beta = beta_of(section * depths + depth, sections * depths)
        kept = residual_scale * upstream
        d_before = (0.5 * kept) * ref[SLOPE][depth, rows, :].astype(jnp.float32)
        d_scaled = (beta * d_before).astype(jnp.bfloat16)
        ref[SCALED][depth, rows, :] = d_scaled
        product = dot_f32(d_scaled, ref[WEIGHTS_T][depth])
        direct = kept + ((1.0 - mix_alpha) * (1.0 - beta)) * d_before
        upstream = direct + (1.0 - mix_alpha) * product
    grad = upstream.astype(jnp.bfloat16)
    if send is not None:
        send[...] = grad
    ref[GRADS][rows, :] = grad


def extra_kernel(slot, sections, per_group, names_in, names_out, *refs):
    refs = list(refs)
    ref = {name: refs.pop(0) for name in names_in}
    ref.update({name: refs.pop(0) for name in names_out})
    ref[INDEX_SMEM], ref[COUNT_SMEM], ref[PLACED], sems = refs
    section = lax.axis_index("section")
    tables = table_copies(ref, sems)
    if slot == 0:
        for copy in tables:
            copy.start()
        for copy in tables:
            copy.wait()
        for stream in range(STREAMS):
            if PHASES[stream]:
                compute_mix(ref, stream, 1, per_group)
        compute_mix(ref, STREAMS, STREAMS, per_group)
        return

    @pl.when(lax.rem(section + slot, 2) == 1)
    def _():
        for copy in tables:
            copy.start()
        if slot == 2:
            cotangent = pltpu.make_async_copy(ref[COTANGENT_HBM], ref[COTANGENT], sems.at[2])

            @pl.when(section == sections - 1)
            def _():
                cotangent.start()

        for copy in tables:
            copy.wait()
        compute_mix(ref, (2 + (slot - 1) // 2) * STREAMS, STREAMS, per_group)
        if slot == 2:

            @pl.when(section == sections - 1)
            def _():
                cotangent.wait()


def turn_kernel(slot, names_in, names_out, *refs):
    ref = dict(zip(names_in + names_out, refs))

    @pl.when(lax.rem(lax.axis_index("section") + slot, 2) == 1)
    def _():
        depths, width, _ = ref[WEIGHTS].shape
        side = 2 * TILE
        blocks = width // side

        @pl.loop(0, depths * blocks * blocks)
        def _(n):
            depth = lax.div(n, blocks * blocks)
            down = pl.ds(pl.multiple_of(lax.rem(lax.div(n, blocks), blocks) * side, side), side)
            along = pl.ds(pl.multiple_of(lax.rem(n, blocks) * side, side), side)
            ref[WEIGHTS_T][depth, along, down] = ref[WEIGHTS][depth, down, along].T


def weight_kernel(slot, step, names_in, names_out, *refs):
    ref = dict(zip(names_in + names_out, refs))
    size = STREAMS * TILE
    rows = slice(step * size, (step + 1) * size)

    @pl.when(lax.rem(lax.axis_index("section") + slot, 2) == 0)
    def _():
        if step == 0:
            copy = pltpu.make_async_copy(ref[STATES], ref[STATES_OUT], refs[-1])
            copy.start()

        @pl.loop(0, ref[TOTAL].shape[0])
        def _(depth):
            term = dot_t(ref[ROUNDED][depth, rows, :], ref[SCALED][depth, rows, :])
            if step == 0:
                ref[TOTAL][depth] = term
            else:
                ref[TOTAL][depth] += term

        if step == 0:
            copy.wait()


def tick_kernel(plan, depths, per_group, names_in, names_out, *refs):
    refs = list(refs)
    recv = refs.pop(0) if plan.tick else None
    ref = {name: refs.pop(0) for name in names_in}
    send = None if plan.last else refs.pop(0)
    ref.update({name: refs.pop(0) for name in names_out})
    if plan.first_mix:
        ref[INDEX_SMEM], ref[COUNT_SMEM], ref[PLACED] = refs.pop(0), refs.pop(0), refs.pop(0)
    sems = refs.pop(0) if refs else None
    section = lax.axis_index("section")
    sections, tick, stream = plan.sections, plan.tick, plan.stream
    own = lax.rem(section + tick, 2) == 0

    if plan.first_mix:
        tables = table_copies(ref, sems)
        for copy in tables:
            copy.start()
    group = per_group * TILE
    rest = []
    if plan.load_rest:
        items = ref[TILES].shape[0]
        spare, others = pl.ds(group, (items - 1) * group), pl.ds(1, items - 1)
        rest = [
            pltpu.make_async_copy(ref[TILES_HBM].at[others], ref[TILES].at[others], sems.at[2]),
            pltpu.make_async_copy(ref[FEATURES_HBM].at[spare], ref[FEATURES].at[spare], sems.at[3]),
        ]
        for copy in rest:
            copy.start()
    if plan.load_first:
        item = pl.ds(0, group)
        first = [
            pltpu.make_async_copy(ref[TILES_HBM].at[0], ref[TILES].at[0], sems.at[2]),
            pltpu.make_async_copy(ref[STALE_HBM], ref[STALE], sems.at[3]),
            pltpu.make_async_copy(ref[FEATURES_HBM].at[item], ref[FEATURES].at[item], sems.at[4]),
            pltpu.make_async_copy(ref[WEIGHTS_HBM], ref[WEIGHTS], sems.at[5]),
        ]
        for copy in first:
            copy.start()
        for copy in first[:3]:
            copy.wait()
    if plan.first_mix:
        for copy in tables:
            copy.wait()
        compute_mix(ref, stream, 1, per_group)
    if plan.load_first:
        first[3].wait()

    def rows_of(step):
        return pl.ds(pl.multiple_of((step * STREAMS + stream) * TILE, TILE), TILE)

    if plan.forward:
        twice = tick - section

        @pl.when(own & (twice >= 0) & (twice < 2 * plan.steps))
        def _():
            forward_chunk(ref, rows_of(lax.div(twice, 2)), section, sections, recv, send)

    if plan.backward:
        twice_back = tick - (2 * sections - 1) + section

        @pl.when(jnp.logical_not(own) & (twice_back >= 0) & (twice_back < 2 * plan.steps))
        def _():
            rows = rows_of(lax.div(twice_back, 2))
            backward_chunk(ref, rows, section, sections, recv, send)

    for copy in rest:
        copy.wait()


def finish_kernel(rows, reps, rounded, scaled, total, grads, keep, give, grads_out, sem):
    copy = pltpu.make_async_copy(grads, grads_out, sem)
    copy.start()
    depths, width, _ = total.shape
    share = width // reps
    core = lax.rem(lax.axis_index("rep"), 2)

    @pl.loop(0, depths)
    def _(depth):
        term = dot_t(rounded[depth, rows, :], scaled[depth, rows, :])
        full = ((total[depth] + term) * (1.0 / reps)).astype(jnp.bfloat16)
        for q in range(reps // 2):
            even = full[2 * q * share : (2 * q + 1) * share, :]
            odd = full[(2 * q + 1) * share : (2 * q + 2) * share, :]
            place = pl.ds(pl.multiple_of((q * depths + depth) * share, share), share)
            keep[place, :] = jnp.where(core == 0, even, odd)
            give[place, :] = jnp.where(core == 0, odd, even)

    copy.wait()


def spec_of(name):
    space = pltpu.HBM if name in IN_HBM else pltpu.VMEM
    return pl.BlockSpec(memory_space=space)


def body(features, stale_states, tile_values, tile_index, tile_count, weights, cotangent):
    sections = lax.axis_size("section")
    reps = lax.axis_size("rep")
    depths = weights.shape[0]
    nodes, width = features.shape
    per_group = tile_values.shape[2]
    steps = nodes // (STREAMS * TILE)
    ticks = 2 * sections - 2 + 2 * steps

    buffers = {
        FEATURES_HBM: features,
        STALE_HBM: stale_states,
        TILES_HBM: tile_values,
        WEIGHTS_HBM: weights,
        COTANGENT_HBM: cotangent,
        INDEX_HBM: jnp.swapaxes(tile_index, 2, 3),
        COUNT_HBM: tile_count,
    }
    low, wide = jnp.bfloat16, jnp.float32
    struct = jax.ShapeDtypeStruct
    shapes = {
        FEATURES: struct(features.shape, low),
        STALE: struct(stale_states.shape, low),
        TILES: struct(tile_values.shape, low),
        WEIGHTS: struct(weights.shape, low),
        WEIGHTS_T: struct(weights.shape, low),
        COTANGENT: struct(cotangent.shape, low),
        MIX: struct((depths, nodes, width), wide),
        SLOPE: struct((depths, nodes, width), low),
        ROUNDED: struct((depths, nodes, width), low),
        SCALED: struct((depths, nodes, width), low),
        STATES: struct((nodes, width), low),
        STATES_OUT: struct((nodes, width), low),
        GRADS: struct((nodes, width), low),
        TOTAL: struct((depths, width, width), wide),
    }
    parcel = struct((TILE, width), low)
    exchange = [
        [(i, i ^ 1) for i in range(sections)],
        [((i + 1) % sections, ((i ^ 1) + 1) % sections) for i in range(sections)],
    ]
    tables = [pltpu.SMEM(buffers[n].shape, jnp.int32) for n in (INDEX_HBM, COUNT_HBM)]
    tables.append(pltpu.VMEM((STREAMS * TILE, stale_states.shape[1]), low))

    def call(kernel, name, reads, writes, mail_in, mail_out, scratch):
        names_out = sorted(writes)
        names_in = sorted((reads | writes) & set(buffers))
        operands = [
            pltpu.with_memory_space_constraint(buffers[n], pltpu.HBM) if n in ARGS_HBM else buffers[n]
            for n in names_in
        ]
        results = pl.pallas_call(
            functools.partial(kernel, names_in, names_out),
            out_shape=mail_out + [shapes[n] for n in names_out],
            in_specs=[spec_of(None) for _ in mail_in] + [spec_of(n) for n in names_in],
            out_specs=[spec_of(None) for _ in mail_out] + [spec_of(n) for n in names_out],
            scratch_shapes=scratch,
            input_output_aliases={
                len(mail_in) + names_in.index(n): len(mail_out) + names_out.index(n)
                for n in names_out
                if n in buffers
            },
            compiler_params=pltpu.CompilerParams(vmem_limit_bytes=GRANT),
            cost_estimate=pl.CostEstimate(
                flops=4 * TILE * width * width, bytes_accessed=1 << 20, transcendentals=0
            ),
            name=name,
        )(*mail_in, *operands)
        buffers.update(zip(names_out, results[len(mail_out) :]))
        return results[: len(mail_out)]

    received = [None] * STREAMS
    for slot in range(ticks + max(PHASES)):
        for stream, phase in enumerate(PHASES):
            tick = slot - phase
            if not 0 <= tick < ticks:
                continue
            plan = Plan(tick, stream, sections, steps)
            mail_in = [received[stream]] if tick else []
            mail_out = [] if plan.last else [parcel]
            scratch = list(tables) if plan.first_mix else []
            if plan.first_mix:
                scratch.append(pltpu.SemaphoreType.DMA((6,)))
            sent = call(
                functools.partial(tick_kernel, plan, depths, per_group),
                f"tick{tick}_{stream}",
                plan.reads,
                plan.writes,
                mail_in,
                mail_out,
                scratch,
            )
            if not plan.last:
                received[stream] = lax.ppermute(sent[0], "section", exchange[tick % 2])
        if slot <= 2 * (steps - 2):
            call(
                functools.partial(extra_kernel, slot, sections, per_group),
                f"mix{slot}",
                {INDEX_HBM, COUNT_HBM, FEATURES, STALE, TILES} | ({COTANGENT_HBM} if slot == 2 else set()),
                {MIX, STATES} | ({COTANGENT} if slot == 2 else set()),
                [],
                [],
                tables + [pltpu.SemaphoreType.DMA((3,))],
            )
        if slot in (sections - 3, sections - 2):
            call(
                functools.partial(turn_kernel, slot), f"turn{slot}", {WEIGHTS}, {WEIGHTS_T, STATES}, [], [], []
            )
        step = (slot - 2 * sections) // 2
        if 0 <= step < steps - 1:
            call(
                functools.partial(weight_kernel, slot, step),
                f"weight{slot}",
                {ROUNDED, STATES} if step == 0 else {ROUNDED},
                {TOTAL, SCALED, GRADS} | ({STATES_OUT} if step == 0 else set()),
                [],
                [],
                [pltpu.SemaphoreType.DMA] if step == 0 else [],
            )

    size = STREAMS * TILE
    half = struct((depths * width // 2, width), low)
    keep, give, grads_out = pl.pallas_call(
        functools.partial(finish_kernel, slice((steps - 1) * size, steps * size), reps),
        out_shape=[half, half, shapes[GRADS]],
        in_specs=[spec_of(None)] * 4,
        out_specs=[spec_of(None)] * 2 + [pl.BlockSpec(memory_space=pltpu.HBM)],
        scratch_shapes=[pltpu.SemaphoreType.DMA],
        compiler_params=pltpu.CompilerParams(vmem_limit_bytes=GRANT),
        name="finish",
    )(buffers[ROUNDED], buffers[SCALED], buffers[TOTAL], buffers[GRADS])
    got = lax.ppermute(give, "rep", [(i, i ^ 1) for i in range(reps)])
    chip = (keep.astype(wide) + got.astype(wide)).astype(low)
    parts = lax.all_to_all(
        chip.reshape(reps // 2, -1, width),
        "rep",
        split_axis=0,
        concat_axis=0,
        tiled=True,
        axis_index_groups=[list(range(core, reps, 2)) for core in range(2)],
    )
    weight_grads = parts.astype(wide).sum(0)
    return (
        buffers[STATES_OUT][None],
        grads_out[None],
        weight_grads.reshape(depths, width // reps, width),
    )


def solution(mesh):
    return jax.shard_map(
        body,
        mesh=mesh,
        in_specs=(
            P("rep", None),
            P("section", "rep", None),
            P("rep", None, None, None, None, None),
            P("rep", None, None, None),
            P("rep", None, None),
            P("section", None, None),
            P("rep", None),
        ),
        out_specs=(P("section", "rep", None), P("section", "rep", None), P("section", "rep", None)),
        check_vma=False,
    )
```
